32 devices in a mesh: face: 4 (over x, core), tile: 8 (over z, y).
Axes of the slice: x: 2, y: 2, z: 4, core: 2. Of those that a mesh axis runs over, the one named last changes fastest.
Arguments:
- field_in: bfloat16 [12, 48, 256, 256], P('face', None, 'tile'), may hold values from -6 to 6
- out_grad: bfloat16 [12, 48, 256, 256], P('face', None, 'tile'), may hold values from -6 to 6
- weight_first: bfloat16 [48, 48, 3, 3], replicated, may hold values from -0.3125 to 0.3125
- bias_first: float32 [48], replicated, may hold values from -3 to 3
- weight_second: bfloat16 [48, 48, 3, 3], replicated, may hold values from -0.3125 to 0.3125
- bias_second: float32 [48], replicated, may hold values from -3 to 3
- face_links: int32 [12, 4, 3], replicated, may hold values from 0 to 11, as said below
- corner_rules: int32 [12, 4], replicated, may hold values from 0 to 1
Outputs:
- output_field: bfloat16 [12, 48, 256, 256], P('face', None, 'tile')
- grad_field: bfloat16 [12, 48, 256, 256], P('face', None, 'tile')
- grad_weight_first: float32 [48, 48, 3, 3], replicated
- grad_bias_first: float32 [48], replicated
- grad_weight_second: float32 [48, 48, 3, 3], replicated
- grad_bias_second: float32 [48], replicated
The draws below stay inside these ranges and needn't reach their ends.
Inputs may be any that keep to these rules, and one draw needn't show every extreme that they name: face_links[f, e] = (g, e2, r) glues edge e of face f to edge e2 of face g; r = 1 when positions along the two edges run in opposite directions. The gluing is a pairing: (g, e2) differs from (f, e) and face_links[g, e2] = (f, e, r). The partner face lies in 0..11, the edge in 0..3, the flag in 0..1.
All inputs are finite; a program needn't handle non-finite values.
Results may differ from the reference program's by a relative error of at most 0.0055.
The reference program's roundings to bfloat16 on the way count: a program that leaves them out, or rounds other values in their place, can miss the bound.
Values may be sent and summed in bfloat16 or wider, within the bound.
A program may use at most 256 MiB of HBM per device.

```python
import jax
import jax.numpy as jnp
from jax import lax

C = 48
FACES = 12
NSIDE = 256


def draw_face_links(key, part):
    order = jax.random.permutation(key, 4 * FACES).astype(jnp.int32)
    flips = jax.random.randint(jax.random.fold_in(key, 7), (2 * FACES,), 0, 2).astype(jnp.int32)
    first_edge = order[0::2]
    second_edge = order[1::2]
    table = jnp.zeros((4 * FACES, 3), jnp.int32)
    table = table.at[first_edge].set(jnp.stack([second_edge // 4, second_edge % 4, flips], axis=1))
    table = table.at[second_edge].set(jnp.stack([first_edge // 4, first_edge % 4, flips], axis=1))
    return table.reshape(FACES, 4, 3)


def with_ends(result, rng, low, high):
    longest = result.shape.index(max(result.shape))
    spots = []
    for shift in (0, 1):
        where = [jax.random.randint(jax.random.fold_in(rng, axis), (), 0, length) for axis, length in enumerate(result.shape)]
        where[longest] = (where[longest] + shift) % result.shape[longest]
        spots.append(tuple(where))
    return result.at[spots[0]].set(low).at[spots[1]].set(high)


def block_levels(own_key, shape, split, smallest, largest):
    gain = 1.0
    for position, parts in split:
        heights = jax.random.uniform(jax.random.fold_in(jax.random.fold_in(own_key, 6), position), (parts,), jnp.float32, smallest / len(split), largest / len(split))
        gain = gain * jnp.repeat(jnp.exp(heights), shape[position] // parts).reshape((-1,) + (1,) * (len(shape) - 1 - position))
    return gain


def gaussian(key, extent, width, most, shards=(), held_as=jnp.bfloat16):
    result = width * jax.random.normal(key, extent, jnp.float32)
    if shards:
        result = result * block_levels(key, extent, shards, -0.22, 0.18)
    return jnp.clip(result, -most, most).astype(held_as)


def setup_inputs(seed: int = 0) -> dict:
    seeds = jax.random.split(jax.random.key(seed), 9)
    field_in = gaussian(seeds[0], (FACES, C, NSIDE, NSIDE), 1.0, 6.0, ((0, 4), (2, 8)))
    out_grad = gaussian(seeds[1], (FACES, C, NSIDE, NSIDE), 1.0, 6.0, ((0, 4), (2, 8)))
    weight_first = gaussian(seeds[2], (C, C, 3, 3), (9 * C) ** -0.5, 0.3125)
    bias_first = gaussian(seeds[3], (C,), 0.5, 3.0, (), jnp.float32)
    weight_second = gaussian(seeds[4], (C, C, 3, 3), (9 * C) ** -0.5, 0.3125)
    bias_second = gaussian(seeds[5], (C,), 0.5, 3.0, (), jnp.float32)
    face_links = draw_face_links(jax.random.fold_in(seeds[8], 71), 0)
    corner_rules = with_ends(jax.random.randint(seeds[7], (FACES, 4), 0, 2), jax.random.fold_in(seeds[7], 1), 0, 1).astype(jnp.int32)
    return {"field_in": field_in, "out_grad": out_grad, "weight_first": weight_first, "bias_first": bias_first, "weight_second": weight_second, "bias_second": bias_second, "face_links": face_links, "corner_rules": corner_rules}


INV_ROOT_TWO = 0.7071067811865476
INV_ROOT_TWO_PI = 0.3989422804014327

def gelu_pair(values):
    normal_cdf = 0.5 * (1.0 + lax.erf(values * INV_ROOT_TWO))
    normal_pdf = jnp.exp(-0.5 * values * values) * INV_ROOT_TWO_PI
    return (values * normal_cdf, normal_cdf + values * normal_pdf)

def convolve(padded, weight):
    return lax.conv_general_dilated(padded.astype(jnp.float32), weight.astype(jnp.float32), (1, 1), 'VALID', dimension_numbers=('NCHW', 'OIHW', 'NCHW'), precision=lax.Precision.HIGHEST)

def edge_lines(activation):
    return jnp.stack([activation[:, :, 0, :], activation[:, :, -1, :], activation[:, :, :, 0], activation[:, :, :, -1]], axis=1)

def partner(lines_all, face_links):
    source = lines_all[face_links[:, :, 0], face_links[:, :, 1]]
    flipped = source[..., ::-1]
    return jnp.where((face_links[:, :, 2] == 1)[:, :, None, None], flipped, source)

def fill_seams(activation, face_links, corner_rules):
    ghosts = partner(edge_lines(activation), face_links)
    north_line, south_line, west_line, east_line = (ghosts[:, 0], ghosts[:, 1], ghosts[:, 2], ghosts[:, 3])
    corner_code = (corner_rules == 0)[:, :, None]
    corner_nw = jnp.where(corner_code[:, 0], north_line[:, :, 0], west_line[:, :, 0])
    corner_ne = jnp.where(corner_code[:, 1], north_line[:, :, -1], east_line[:, :, 0])
    corner_sw = jnp.where(corner_code[:, 2], south_line[:, :, 0], west_line[:, :, -1])
    corner_se = jnp.where(corner_code[:, 3], south_line[:, :, -1], east_line[:, :, -1])
    middle = jnp.concatenate([west_line[:, :, :, None], activation, east_line[:, :, :, None]], axis=3)
    top_row = jnp.concatenate([corner_nw[:, :, None], north_line, corner_ne[:, :, None]], axis=2)
    bottom_row = jnp.concatenate([corner_sw[:, :, None], south_line, corner_se[:, :, None]], axis=2)
    return jnp.concatenate([top_row[:, :, None], middle, bottom_row[:, :, None]], axis=2)

def back_conv(cotangent, weight):
    padded = jnp.pad(cotangent, ((0, 0), (0, 0), (2, 2), (2, 2)))
    flipped = jnp.transpose(weight[:, :, ::-1, ::-1], (1, 0, 2, 3))
    return convolve(padded, flipped)

def unfold(pad_grad, face_links, corner_rules):
    north_line = pad_grad[:, :, 0, 1:-1]
    south_line = pad_grad[:, :, -1, 1:-1]
    west_line = pad_grad[:, :, 1:-1, 0]
    east_line = pad_grad[:, :, 1:-1, -1]
    corner_nw = pad_grad[:, :, 0, 0]
    corner_ne = pad_grad[:, :, 0, -1]
    corner_sw = pad_grad[:, :, -1, 0]
    corner_se = pad_grad[:, :, -1, -1]
    corner_code = corner_rules[:, :, None]
    zero = jnp.float32(0.0)
    north_line = north_line.at[:, :, 0].add(jnp.where(corner_code[:, 0] == 0, corner_nw, zero))
    north_line = north_line.at[:, :, -1].add(jnp.where(corner_code[:, 1] == 0, corner_ne, zero))
    south_line = south_line.at[:, :, 0].add(jnp.where(corner_code[:, 2] == 0, corner_sw, zero))
    south_line = south_line.at[:, :, -1].add(jnp.where(corner_code[:, 3] == 0, corner_se, zero))
    west_line = west_line.at[:, :, 0].add(jnp.where(corner_code[:, 0] == 1, corner_nw, zero))
    west_line = west_line.at[:, :, -1].add(jnp.where(corner_code[:, 2] == 1, corner_sw, zero))
    east_line = east_line.at[:, :, 0].add(jnp.where(corner_code[:, 1] == 1, corner_ne, zero))
    east_line = east_line.at[:, :, -1].add(jnp.where(corner_code[:, 3] == 1, corner_se, zero))
    lines_grad = jnp.stack([north_line, south_line, west_line, east_line], axis=1).astype(jnp.bfloat16)
    returned = partner(lines_grad, face_links).astype(jnp.float32)
    interior = pad_grad[:, :, 1:-1, 1:-1]
    interior = interior.at[:, :, 0, :].add(returned[:, 0])
    interior = interior.at[:, :, -1, :].add(returned[:, 1])
    interior = interior.at[:, :, :, 0].add(returned[:, 2])
    interior = interior.at[:, :, :, -1].add(returned[:, 3])
    return interior

def weight_grad(cotangent, padded):
    row_count, col_count = (cotangent.shape[2], cotangent.shape[3])
    channels = cotangent.shape[1]
    grad_wide = cotangent.astype(jnp.float32)
    products = []
    for row_off in range(3):
        for col_off in range(3):
            window = padded[:, :, row_off:row_off + row_count, col_off:col_off + col_count].astype(jnp.float32)
            products.append(jnp.einsum('ncrs,nirs->ci', grad_wide, window, precision=lax.Precision.HIGHEST))
    return jnp.stack(products).reshape(3, 3, channels, channels).transpose(2, 3, 0, 1)

def reference(field_in, out_grad, weight_first, bias_first, weight_second, bias_second, face_links, corner_rules):
    padded_first = fill_seams(field_in, face_links, corner_rules)
    pre_first = convolve(padded_first, weight_first) + bias_first[None, :, None, None]
    gelu_first, slope_first = gelu_pair(pre_first)
    hidden = gelu_first.astype(jnp.bfloat16)
    padded_second = fill_seams(hidden, face_links, corner_rules)
    pre_second = convolve(padded_second, weight_second) + bias_second[None, :, None, None]
    gelu_second, slope_second = gelu_pair(pre_second)
    output_field = gelu_second.astype(jnp.bfloat16)
    grad_second = (out_grad.astype(jnp.float32) * slope_second).astype(jnp.bfloat16)
    grad_weight_second = weight_grad(grad_second, padded_second) / NSIDE
    grad_bias_second = lax.optimization_barrier(jnp.sum(grad_second.astype(jnp.float32), axis=(0, 2, 3))) / NSIDE
    grad_hidden = unfold(back_conv(grad_second, weight_second), face_links, corner_rules)
    grad_first = (grad_hidden * slope_first).astype(jnp.bfloat16)
    grad_weight_first = weight_grad(grad_first, padded_first) / NSIDE
    grad_bias_first = lax.optimization_barrier(jnp.sum(grad_first.astype(jnp.float32), axis=(0, 2, 3))) / NSIDE
    grad_field = unfold(back_conv(grad_first, weight_first), face_links, corner_rules).astype(jnp.bfloat16)
    return (output_field, grad_field, grad_weight_first, grad_bias_first, grad_weight_second, grad_bias_second)
```

```python
import functools

import jax
import jax.numpy as jnp
from jax import lax
from jax.experimental import pallas as pl
from jax.experimental.pallas import tpu as pltpu
from jax.sharding import PartitionSpec as P

INV_ROOT_TWO = 0.7071067811865476
INV_ROOT_TWO_PI = 0.3989422804014327
F32 = jnp.float32
BF16 = jnp.bfloat16
LANES = 128
MESH_ID = pl.DeviceIdType.MESH


def gelu_pair(values):
    normal_cdf = 0.5 * (1.0 + lax.erf(values * INV_ROOT_TWO))
    normal_pdf = jnp.exp(-0.5 * values * values) * INV_ROOT_TWO_PI
    return (values * normal_cdf, normal_cdf + values * normal_pdf)


def lane_index(channels):
    return lax.broadcasted_iota(jnp.int32, (channels, LANES), 1)


def build_patches(x_ref, halo_ref, ghost_ref, patch_ref):
    rows, channels, width = x_ref.shape
    lane = lane_index(channels)

    def put(p, row):
        wide = row.astype(F32)
        left = pltpu.roll(wide, 1, 1)
        right = pltpu.roll(wide, width - 1, 1)
        if ghost_ref is None:
            west = east = jnp.zeros((channels, LANES), F32)
        else:
            west = pltpu.roll(ghost_ref[0], lax.rem(LANES - p, LANES), 1)
            east = pltpu.roll(ghost_ref[1], LANES - 1 - p, 1)
        left = jnp.concatenate([jnp.where(lane == 0, west, left[:, :LANES]), left[:, LANES:]], axis=1)
        right = jnp.concatenate(
            [right[:, :-LANES], jnp.where(lane == LANES - 1, east, right[:, -LANES:])], axis=1
        )
        patch_ref[p, 0:channels] = left.astype(BF16)
        patch_ref[p, channels : 2 * channels] = row
        patch_ref[p, 2 * channels : 3 * channels] = right.astype(BF16)

    put(jnp.int32(0), halo_ref[0])
    put(jnp.int32(rows + 1), halo_ref[1])

    def step(r, carry):
        for i in range(2):
            put(2 * r + i + 1, x_ref[2 * r + i])
        return carry

    lax.fori_loop(0, rows // 2, step, 0)


def patch_rows(patch_ref, r):
    _, depth, width = patch_ref.shape
    return patch_ref[pl.ds(r, 3)].reshape(3 * depth, width)


def conv_row(w, patch_ref, r):
    return jnp.dot(w, patch_rows(patch_ref, r), preferred_element_type=F32)


def keep_columns(edge_ref, r, row, lane):
    channels, width = row.shape
    edge_ref[0] = jnp.where(lane == r, pltpu.roll(row[:, :LANES], r, 1), edge_ref[0])
    edge_ref[1] = jnp.where(
        lane == r, pltpu.roll(row[:, -LANES:], lax.rem(r + 1, LANES), 1), edge_ref[1]
    )


def over_rows(rows, body):
    group = 4

    def step(s, carry):
        for i in range(group):
            body(s * group + i)
        return carry

    lax.fori_loop(0, rows // group, step, 0)


def first_kernel(x_ref, halo_ref, ghost_ref, w_ref, b_ref, hidden_ref, slope_ref, edge_ref, patch_ref):
    rows, channels, width = x_ref.shape
    build_patches(x_ref, halo_ref, ghost_ref, patch_ref)
    edge_ref[...] = jnp.zeros_like(edge_ref)
    lane = lane_index(channels)
    w = w_ref[...]

    def body(r):
        pre = conv_row(w, patch_ref, r) + b_ref[...]
        value, slope = gelu_pair(pre)
        slope_ref[r] = slope
        hidden_ref[r] = value.astype(BF16)
        keep_columns(edge_ref, r, value, lane)

    over_rows(rows, body)


def add_products(gw_ref, g_row, patch_ref, r):
    gw_ref[...] += lax.dot_general(
        patch_rows(patch_ref, r), g_row, (((1,), (1,)), ((), ())), preferred_element_type=F32
    )


def second_kernel(
    x_ref, halo_ref, ghost_ref, og_ref, w_ref, b_ref, out_ref, g_ref, edge_ref, gw_ref, gb_ref, patch_ref
):
    rows, channels, width = x_ref.shape
    build_patches(x_ref, halo_ref, ghost_ref, patch_ref)
    edge_ref[...] = jnp.zeros_like(edge_ref)

    @pl.when(pl.program_id(0) == 0)
    def _():
        gw_ref[...] = jnp.zeros_like(gw_ref)
        gb_ref[...] = jnp.zeros_like(gb_ref)

    lane = lane_index(channels)
    w = w_ref[...]

    def body(r):
        pre = conv_row(w, patch_ref, r) + b_ref[...]
        value, slope = gelu_pair(pre)
        out_ref[r] = value.astype(BF16)
        grad = (og_ref[r].astype(F32) * slope).astype(BF16)
        g_ref[r] = grad
        wide = grad.astype(F32)
        gb_ref[...] += wide
        keep_columns(edge_ref, r, wide, lane)
        add_products(gw_ref, grad, patch_ref, r)

    over_rows(rows, body)


def add_edges(total, r, rows, col_ref, row_ref, lane):
    west = pltpu.roll(col_ref[0], lax.rem(LANES - r, LANES), 1)
    east = pltpu.roll(col_ref[1], LANES - 1 - r, 1)
    zero = jnp.zeros_like(west)
    parts = [total[:, i : i + LANES] for i in range(0, total.shape[1], LANES)]
    parts[0] = parts[0] + jnp.where(lane == 0, west, zero)
    parts[-1] = parts[-1] + jnp.where(lane == LANES - 1, east, zero)
    total = jnp.concatenate(parts, axis=1)
    north = jnp.where(r == 0, row_ref[0], jnp.zeros_like(row_ref[0]))
    south = jnp.where(r == rows - 1, row_ref[1], jnp.zeros_like(row_ref[1]))
    return total + north + south


def third_kernel(
    g_ref, halo_ref, col_ref, row_ref, slope_ref, x_ref, xhalo_ref, xghost_ref, w_ref,
    out_ref, edge_ref, gw_ref, gb_ref, patch_ref, xpatch_ref,
):
    rows, channels, width = g_ref.shape
    build_patches(g_ref, halo_ref, None, patch_ref)
    build_patches(x_ref, xhalo_ref, xghost_ref, xpatch_ref)
    edge_ref[...] = jnp.zeros_like(edge_ref)

    @pl.when(pl.program_id(0) == 0)
    def _():
        gw_ref[...] = jnp.zeros_like(gw_ref)
        gb_ref[...] = jnp.zeros_like(gb_ref)

    lane = lane_index(channels)
    w = w_ref[...]

    def body(r):
        total = add_edges(conv_row(w, patch_ref, r), r, rows, col_ref, row_ref, lane)
        grad = (total * slope_ref[r]).astype(BF16)
        out_ref[r] = grad
        wide = grad.astype(F32)
        gb_ref[...] += wide
        keep_columns(edge_ref, r, wide, lane)
        add_products(gw_ref, grad, xpatch_ref, r)

    over_rows(rows, body)


def fourth_kernel(g_ref, halo_ref, col_ref, row_ref, w_ref, out_ref, patch_ref):
    rows, channels, width = g_ref.shape
    build_patches(g_ref, halo_ref, None, patch_ref)
    lane = lane_index(channels)
    w = w_ref[...]

    def body(r):
        total = add_edges(conv_row(w, patch_ref, r), r, rows, col_ref, row_ref, lane)
        out_ref[r] = total.astype(BF16)

    over_rows(rows, body)


def per_face(shape):
    tail = len(shape) - 1
    return pl.BlockSpec((None,) + tuple(shape[1:]), lambda f: (f,) + (0,) * tail)


def whole(shape):
    return pl.BlockSpec(tuple(shape), lambda f: (0,) * len(shape))


def run_faces(kernel, faced, shared, faced_outs, shared_outs, patches, flops):
    faces = faced[0].shape[0]
    rows, channels, width = faced[0].shape[1:]
    outs = [jax.ShapeDtypeStruct(s, d) for s, d in faced_outs + shared_outs]
    return pl.pallas_call(
        kernel,
        grid=(faces,),
        in_specs=[per_face(a.shape) for a in faced] + [whole(a.shape) for a in shared],
        out_specs=[per_face(s) for s, _ in faced_outs] + [whole(s) for s, _ in shared_outs],
        out_shape=outs,
        scratch_shapes=[pltpu.VMEM((rows + 2, 3 * channels, width), BF16)] * patches,
        compiler_params=pltpu.CompilerParams(vmem_limit_bytes=40 << 20),
        cost_estimate=pl.CostEstimate(flops=flops, bytes_accessed=10**7, transcendentals=10**6),
    )(*faced, *shared)


def flipped_bit(i, bit):
    return i + bit - 2 * bit * lax.rem(lax.div(i, bit), 2)


def gather_kernel(faces, tiles, we_ref, ns_ref, we_all, ns_all, tsend, trecv, nsend, nrecv, fsend, frecv, gsend, grecv):
    face = lax.axis_index("face")
    tile = lax.axis_index("tile")
    tile_bits = [1 << b for b in range(tiles.bit_length() - 1)]
    face_bits = [1 << b for b in reversed(range(faces.bit_length() - 1))]
    barrier = pltpu.get_barrier_semaphore()
    for bit in tile_bits:
        pl.semaphore_signal(barrier, inc=1, device_id=(face, flipped_bit(tile, bit)), device_id_type=MESH_ID)
    for bit in face_bits:
        pl.semaphore_signal(barrier, inc=1, device_id=(flipped_bit(face, bit), tile), device_id_type=MESH_ID)
    we_all[face, tile] = we_ref[...]

    @pl.when(tile == 0)
    def _():
        ns_all[face, 0] = ns_ref[0]

    @pl.when(tile == tiles - 1)
    def _():
        ns_all[face, 1] = ns_ref[1]

    pl.semaphore_wait(barrier, len(tile_bits) + len(face_bits))
    for i, bit in enumerate(tile_bits):
        partner = (face, flipped_bit(tile, bit))
        block = we_all.at[face, pl.ds(lax.div(tile, bit) * bit, bit)]
        copy = pltpu.make_async_remote_copy(block, block, tsend.at[i], trecv.at[i], partner, MESH_ID)
        copy.start()
        lines = []
        for side, place in enumerate((tile, tiles - 1 - tile)):
            line = ns_all.at[face, side]
            send = pltpu.make_async_remote_copy(
                line, line, nsend.at[side, i], nrecv.at[side, i], partner, MESH_ID
            )
            lines.append((place, send))

            @pl.when(place < bit)
            def _():
                send.start()

        copy.wait()
        for place, send in lines:

            @pl.when(place < bit)
            def _():
                send.wait_send()

            @pl.when((place >= bit) & (place < 2 * bit))
            def _():
                send.wait_recv()

    held = [face]
    slot = 0
    for bit in face_bits:
        partner = (flipped_bit(face, bit), tile)
        copies = []
        for h in held:
            block = we_all.at[h]
            copies.append(pltpu.make_async_remote_copy(block, block, fsend.at[slot], frecv.at[slot], partner, MESH_ID))
            lines = ns_all.at[h]
            copies.append(pltpu.make_async_remote_copy(lines, lines, gsend.at[slot], grecv.at[slot], partner, MESH_ID))
            slot += 1
        for copy in copies:
            copy.start()
        for copy in copies:
            copy.wait()
        held = held + [flipped_bit(h, bit) for h in held]


def gather_lines(we, ns):
    faces, tiles = lax.axis_size("face"), lax.axis_size("tile")
    steps = tiles.bit_length() - 1
    dma = pltpu.SemaphoreType.DMA
    return pl.pallas_call(
        functools.partial(gather_kernel, faces, tiles),
        in_specs=[pl.BlockSpec(memory_space=pltpu.VMEM)] * 2,
        out_specs=[pl.BlockSpec(memory_space=pltpu.VMEM)] * 2,
        out_shape=[
            jax.ShapeDtypeStruct((faces, tiles) + we.shape, BF16),
            jax.ShapeDtypeStruct((faces,) + ns.shape, BF16),
        ],
        scratch_shapes=[
            dma((steps,)), dma((steps,)), dma((2, steps)), dma((2, steps)),
            dma((faces,)), dma((faces,)), dma((faces,)), dma((faces,)),
        ],
        compiler_params=pltpu.CompilerParams(collective_id=0, has_side_effects=True),
    )(we, ns)


def exchange(north, south, west, east, links):
    faces_dev, channels, side = north.shape
    seg = west.shape[2]
    we = jnp.stack([west, east], axis=1)
    we = jnp.transpose(we, (2, 0, 1, 3)).reshape(channels, faces_dev * 2 * seg)
    we_all, ns_all = gather_lines(we, jnp.stack([north, south]))
    groups, tiles = we_all.shape[:2]
    we_all = we_all.reshape(groups, tiles, channels, faces_dev, 2, seg)
    we_all = jnp.transpose(we_all, (0, 3, 4, 2, 1, 5)).reshape(groups, faces_dev, 2, channels, side)
    ns_all = jnp.transpose(ns_all, (0, 2, 1, 3, 4))
    lines = jnp.concatenate([ns_all, we_all], axis=2).reshape(groups * faces_dev * 4, channels, side)
    index = (links[:, :, 0] * 4 + links[:, :, 1]).reshape(-1)
    picked = jnp.take(lines, index, axis=0, mode="clip").reshape(faces_dev, 4, channels, side)
    return jnp.where((links[:, :, 2] == 1)[:, :, None, None], picked[..., ::-1], picked)


def halo(first, last):
    count = lax.axis_size("tile")
    down = [(i, i + 1) for i in range(count - 1)]
    up = [(i + 1, i) for i in range(count - 1)]
    return lax.ppermute(last, "tile", down), lax.ppermute(first, "tile", up)


def fill(north, south, west, east, links, corners, pos, count):
    seg = west.shape[2]
    above, below = halo(north, south)
    ghosts = exchange(north, south, west, east, links)
    code = (corners == 0)[:, :, None]
    gn, gs, gw, ge = (ghosts[:, i] for i in range(4))
    nw = jnp.where(code[:, 0], gn[:, :, 0], gw[:, :, 0])
    ne = jnp.where(code[:, 1], gn[:, :, -1], ge[:, :, 0])
    sw = jnp.where(code[:, 2], gs[:, :, 0], gw[:, :, -1])
    se = jnp.where(code[:, 3], gs[:, :, -1], ge[:, :, -1])
    west_all = jnp.concatenate([nw[:, :, None], gw, sw[:, :, None]], axis=2)
    east_all = jnp.concatenate([ne[:, :, None], ge, se[:, :, None]], axis=2)
    columns = jnp.stack([west_all, east_all], axis=1)
    columns = lax.dynamic_slice_in_dim(columns, pos * seg, seg + 2, 3).astype(F32)
    columns = jnp.pad(columns, ((0, 0), (0, 0), (0, 0), (0, LANES - seg - 2)))
    top = jnp.where(pos == 0, gn, above)
    bottom = jnp.where(pos == count - 1, gs, below)
    return jnp.stack([top, bottom], axis=1), columns


def line_product(weights, line):
    size = line.shape[2]
    padded = jnp.pad(line, ((0, 0), (0, 0), (2, 2)))
    stacked = jnp.concatenate([padded[:, :, 2 - t : 2 - t + size + 2] for t in range(3)], axis=1)
    flat = jnp.transpose(weights, (2, 0, 1)).reshape(-1, weights.shape[1])
    return jnp.einsum("kc,fkq->fcq", flat, stacked, preferred_element_type=F32)


def unfold_edges(north, south, west, east, weight, links, corners, pos, count):
    seg = west.shape[2]
    above, below = halo(north, south)
    rows = jnp.stack([above, below], axis=1)
    west = jnp.concatenate([above[:, :, :1], west, below[:, :, :1]], axis=2)
    east = jnp.concatenate([above[:, :, -1:], east, below[:, :, -1:]], axis=2)
    gn = line_product(weight[:, :, 0, :], north)
    gs = line_product(weight[:, :, 2, :], south)
    gw = line_product(weight[:, :, :, 0], west)[:, :, 2:-2]
    ge = line_product(weight[:, :, :, 2], east)[:, :, 2:-2]
    code = corners[:, :, None]
    zero = jnp.zeros((), F32)
    at_top, at_bottom = pos == 0, pos == count - 1
    nw, ne, sw, se = gn[:, :, :1], gn[:, :, -1:], gs[:, :, :1], gs[:, :, -1:]
    keep = lambda i, corner: jnp.where(code[:, i, :, None] == 0, corner, zero)
    give = lambda i, corner, here: jnp.where((code[:, i, :, None] == 1) & here, corner, zero)
    ends = lambda lo, hi, n: jnp.pad(lo, ((0, 0), (0, 0), (0, n - 1))) + jnp.pad(hi, ((0, 0), (0, 0), (n - 1, 0)))
    side = north.shape[2]
    gn_line = gn[:, :, 1:-1] + ends(keep(0, nw), keep(1, ne), side)
    gs_line = gs[:, :, 1:-1] + ends(keep(2, sw), keep(3, se), side)
    gw_line = gw + ends(give(0, nw, at_top), give(2, sw, at_bottom), seg)
    ge_line = ge + ends(give(1, ne, at_top), give(3, se, at_bottom), seg)
    ghosts = exchange(
        gn_line.astype(BF16), gs_line.astype(BF16), gw_line.astype(BF16), ge_line.astype(BF16), links
    ).astype(F32)
    columns = lax.dynamic_slice_in_dim(ghosts[:, 2:], pos * seg, seg, 3)
    columns = jnp.pad(columns, ((0, 0), (0, 0), (0, 0), (0, LANES - seg)))
    edges = jnp.stack(
        [jnp.where(at_top, ghosts[:, 0], zero), jnp.where(at_bottom, ghosts[:, 1], zero)], axis=1
    )
    return rows, columns, edges


def body(field_in, out_grad, weight_first, bias_first, weight_second, bias_second, face_links, corner_rules):
    count = lax.axis_size("tile")
    pos = lax.axis_index("tile")
    face_pos = lax.axis_index("face")
    faces, channels, rows, side = field_in.shape
    links = lax.dynamic_slice_in_dim(face_links, face_pos * faces, faces, 0)
    corners = lax.dynamic_slice_in_dim(corner_rules, face_pos * faces, faces, 0)
    swap = lambda a: jnp.transpose(a, (0, 2, 1, 3))
    ahead = lambda w: jnp.transpose(w, (0, 2, 3, 1)).reshape(channels, 9 * channels)
    behind = lambda w: jnp.transpose(w[:, :, ::-1, ::-1], (1, 2, 3, 0)).reshape(channels, 9 * channels)
    flops = 2 * 9 * channels * channels * faces * rows * side
    full = (faces, rows, channels, side)
    edge_out = ((faces, 2, channels, LANES), F32)
    sums = [((9 * channels, channels), F32), ((channels, side), F32)]

    x = swap(field_in)
    og = swap(out_grad)
    xhalo, xghost = fill(
        field_in[:, :, 0], field_in[:, :, -1], field_in[:, :, :, 0], field_in[:, :, :, -1],
        links, corners, pos, count,
    )
    hidden, slope, hedge = run_faces(
        first_kernel, [x, xhalo, xghost], [ahead(weight_first), bias_first[:, None]],
        [(full, BF16), (full, F32), edge_out], [], 1, flops,
    )

    def sides(edge):
        return edge[:, 0, :, :rows].astype(BF16), edge[:, 1, :, :rows].astype(BF16)

    hhalo, hghost = fill(hidden[:, 0], hidden[:, -1], *sides(hedge), links, corners, pos, count)
    output, g2, gedge, gw2, gb2 = run_faces(
        second_kernel, [hidden, hhalo, hghost, og], [ahead(weight_second), bias_second[:, None]],
        [(full, BF16), (full, BF16), edge_out], sums, 1, 2 * flops,
    )
    ghalo, gcol, grow = unfold_edges(
        g2[:, 0], g2[:, -1], *sides(gedge), weight_second, links, corners, pos, count
    )
    g1, fedge, gw1, gb1 = run_faces(
        third_kernel, [g2, ghalo, gcol, grow, slope, x, xhalo, xghost], [behind(weight_second)],
        [(full, BF16), edge_out], sums, 2, 2 * flops,
    )
    fhalo, fcol, frow = unfold_edges(
        g1[:, 0], g1[:, -1], *sides(fedge), weight_first, links, corners, pos, count
    )
    (grad_field,) = run_faces(
        fourth_kernel, [g1, fhalo, fcol, frow], [behind(weight_first)], [(full, BF16)], [], 1, flops
    )
    packed = jnp.concatenate(
        [gw1, gw2, jnp.sum(gb1, axis=1)[None], jnp.sum(gb2, axis=1)[None]], axis=0
    )
    packed = lax.psum(packed, ("face", "tile")) / side
    depth = 9 * channels
    shaped = lambda g: jnp.transpose(g.reshape(3, 3, channels, channels), (3, 2, 0, 1))
    return (
        swap(output),
        swap(grad_field),
        shaped(packed[:depth]),
        packed[2 * depth],
        shaped(packed[depth : 2 * depth]),
        packed[2 * depth + 1],
    )


def solution(mesh):
    cells = P("face", None, "tile", None)
    return jax.shard_map(
        body,
        mesh=mesh,
        in_specs=(cells, cells, P(), P(), P(), P(), P(), P()),
        out_specs=(cells, cells, P(), P(), P(), P()),
        check_vma=False,
    )
```

```python
import functools

import jax
import jax.numpy as jnp
from jax import lax
from jax.experimental import pallas as pl
from jax.experimental.pallas import tpu as pltpu
from jax.sharding import PartitionSpec as P

INV_ROOT_TWO = 0.7071067811865476
INV_ROOT_TWO_PI = 0.3989422804014327
F32 = jnp.float32
BF16 = jnp.bfloat16
LANES = 128
MESH_ID = pl.DeviceIdType.MESH


def gelu_pair(values):
    normal_cdf = 0.5 * (1.0 + lax.erf(values * INV_ROOT_TWO))
    normal_pdf = jnp.exp(-0.5 * values * values) * INV_ROOT_TWO_PI
    return (values * normal_cdf, normal_cdf + values * normal_pdf)


def lane_index(channels):
    return lax.broadcasted_iota(jnp.int32, (channels, LANES), 1)


def build_patches(x_ref, halo_ref, ghost_ref, patch_ref):
    rows, channels, width = x_ref.shape
    lane = lane_index(channels)

    def put(p, row):
        wide = row.astype(F32)
        left = pltpu.roll(wide, 1, 1)
        right = pltpu.roll(wide, width - 1, 1)
        if ghost_ref is None:
            west = east = jnp.zeros((channels, LANES), F32)
        else:
            west = pltpu.roll(ghost_ref[0], lax.rem(LANES - p, LANES), 1)
            east = pltpu.roll(ghost_ref[1], LANES - 1 - p, 1)
        left = jnp.concatenate([jnp.where(lane == 0, west, left[:, :LANES]), left[:, LANES:]], axis=1)
        right = jnp.concatenate(
            [right[:, :-LANES], jnp.where(lane == LANES - 1, east, right[:, -LANES:])], axis=1
        )
        patch_ref[p, 0:channels] = left.astype(BF16)
        patch_ref[p, channels : 2 * channels] = row
        patch_ref[p, 2 * channels : 3 * channels] = right.astype(BF16)

    put(jnp.int32(0), halo_ref[0])
    put(jnp.int32(rows + 1), halo_ref[1])

    def step(r, carry):
        for i in range(2):
            put(2 * r + i + 1, x_ref[2 * r + i])
        return carry

    lax.fori_loop(0, rows // 2, step, 0)


def patch_rows(patch_ref, r):
    _, depth, width = patch_ref.shape
    return patch_ref[pl.ds(r, 3)].reshape(3 * depth, width)


def conv_row(w, patch_ref, r):
    return jnp.dot(w, patch_rows(patch_ref, r), preferred_element_type=F32)


def keep_columns(edge_ref, r, row, lane):
    channels, width = row.shape
    edge_ref[0] = jnp.where(lane == r, pltpu.roll(row[:, :LANES], r, 1), edge_ref[0])
    edge_ref[1] = jnp.where(
        lane == r, pltpu.roll(row[:, -LANES:], lax.rem(r + 1, LANES), 1), edge_ref[1]
    )


def over_rows(rows, body):
    group = 4

    def step(s, carry):
        for i in range(group):
            body(s * group + i)
        return carry

    lax.fori_loop(0, rows // group, step, 0)


def first_kernel(x_ref, halo_ref, ghost_ref, w_ref, b_ref, hidden_ref, slope_ref, edge_ref, patch_ref):
    rows, channels, width = x_ref.shape
    build_patches(x_ref, halo_ref, ghost_ref, patch_ref)
    edge_ref[...] = jnp.zeros_like(edge_ref)
    lane = lane_index(channels)
    w = w_ref[...]

    def body(r):
        pre = conv_row(w, patch_ref, r) + b_ref[...]
        value, slope = gelu_pair(pre)
        slope_ref[r] = slope
        hidden_ref[r] = value.astype(BF16)
        keep_columns(edge_ref, r, value, lane)

    over_rows(rows, body)


def add_products(gw_ref, g_row, patch_ref, r):
    gw_ref[...] += lax.dot_general(
        patch_rows(patch_ref, r), g_row, (((1,), (1,)), ((), ())), preferred_element_type=F32
    )


def second_kernel(
    x_ref, halo_ref, ghost_ref, og_ref, w_ref, b_ref, out_ref, g_ref, edge_ref, gw_ref, gb_ref, patch_ref
):
    rows, channels, width = x_ref.shape
    build_patches(x_ref, halo_ref, ghost_ref, patch_ref)
    edge_ref[...] = jnp.zeros_like(edge_ref)

    @pl.when(pl.program_id(0) == 0)
    def _():
        gw_ref[...] = jnp.zeros_like(gw_ref)
        gb_ref[...] = jnp.zeros_like(gb_ref)

    lane = lane_index(channels)
    w = w_ref[...]

    def body(r):
        pre = conv_row(w, patch_ref, r) + b_ref[...]
        value, slope = gelu_pair(pre)
        out_ref[r] = value.astype(BF16)
        grad = (og_ref[r].astype(F32) * slope).astype(BF16)
        g_ref[r] = grad
        wide = grad.astype(F32)
        gb_ref[...] += wide
        keep_columns(edge_ref, r, wide, lane)
        add_products(gw_ref, grad, patch_ref, r)

    over_rows(rows, body)


def add_edges(total, r, rows, col_ref, row_ref, lane):
    west = pltpu.roll(col_ref[0], lax.rem(LANES - r, LANES), 1)
    east = pltpu.roll(col_ref[1], LANES - 1 - r, 1)
    zero = jnp.zeros_like(west)
    parts = [total[:, i : i + LANES] for i in range(0, total.shape[1], LANES)]
    parts[0] = parts[0] + jnp.where(lane == 0, west, zero)
    parts[-1] = parts[-1] + jnp.where(lane == LANES - 1, east, zero)
    total = jnp.concatenate(parts, axis=1)
    north = jnp.where(r == 0, row_ref[0], jnp.zeros_like(row_ref[0]))
    south = jnp.where(r == rows - 1, row_ref[1], jnp.zeros_like(row_ref[1]))
    return total + north + south


def third_kernel(
    g_ref, halo_ref, col_ref, row_ref, slope_ref, x_ref, xhalo_ref, xghost_ref, w_ref,
    out_ref, edge_ref, gw_ref, gb_ref, patch_ref, xpatch_ref,
):
    rows, channels, width = g_ref.shape
    build_patches(g_ref, halo_ref, None, patch_ref)
    build_patches(x_ref, xhalo_ref, xghost_ref, xpatch_ref)
    edge_ref[...] = jnp.zeros_like(edge_ref)

    @pl.when(pl.program_id(0) == 0)
    def _():
        gw_ref[...] = jnp.zeros_like(gw_ref)
        gb_ref[...] = jnp.zeros_like(gb_ref)

    lane = lane_index(channels)
    w = w_ref[...]

    def body(r):
        total = add_edges(conv_row(w, patch_ref, r), r, rows, col_ref, row_ref, lane)
        grad = (total * slope_ref[r]).astype(BF16)
        out_ref[r] = grad
        wide = grad.astype(F32)
        gb_ref[...] += wide
        keep_columns(edge_ref, r, wide, lane)
        add_products(gw_ref, grad, xpatch_ref, r)

    over_rows(rows, body)


def fourth_kernel(g_ref, halo_ref, col_ref, row_ref, w_ref, out_ref, patch_ref):
    rows, channels, width = g_ref.shape
    build_patches(g_ref, halo_ref, None, patch_ref)
    lane = lane_index(channels)
    w = w_ref[...]

    def body(r):
        total = add_edges(conv_row(w, patch_ref, r), r, rows, col_ref, row_ref, lane)
        out_ref[r] = total.astype(BF16)

    over_rows(rows, body)


def per_face(shape):
    tail = len(shape) - 1
    return pl.BlockSpec((None,) + tuple(shape[1:]), lambda f: (f,) + (0,) * tail)


def whole(shape):
    return pl.BlockSpec(tuple(shape), lambda f: (0,) * len(shape))


def run_faces(kernel, faced, shared, faced_outs, shared_outs, patches, flops):
    faces = faced[0].shape[0]
    rows, channels, width = faced[0].shape[1:]
    outs = [jax.ShapeDtypeStruct(s, d) for s, d in faced_outs + shared_outs]
    return pl.pallas_call(
        kernel,
        grid=(faces,),
        in_specs=[per_face(a.shape) for a in faced] + [whole(a.shape) for a in shared],
        out_specs=[per_face(s) for s, _ in faced_outs] + [whole(s) for s, _ in shared_outs],
        out_shape=outs,
        scratch_shapes=[pltpu.VMEM((rows + 2, 3 * channels, width), BF16)] * patches,
        compiler_params=pltpu.CompilerParams(vmem_limit_bytes=40 << 20),
        cost_estimate=pl.CostEstimate(flops=flops, bytes_accessed=10**7, transcendentals=10**6),
    )(*faced, *shared)


def flipped_bit(i, bit):
    return i + bit - 2 * bit * lax.rem(lax.div(i, bit), 2)


def gather_kernel(faces, tiles, summed, *refs):
    refs = list(refs)
    we_ref, ns_ref = refs[:2]
    sum_ref = refs[2] if summed else None
    refs = refs[2 + summed :]
    we_all, ns_all = refs[:2]
    total = refs[2] if summed else None
    refs = refs[2 + summed :]
    wsend, wrecv, nsend, nrecv, fsend, frecv = refs[:6]
    landed, ssend, srecv = refs[6:] if summed else (None, None, None)
    face = lax.axis_index("face")
    tile = lax.axis_index("tile")
    tile_bits = [1 << b for b in reversed(range(tiles.bit_length() - 1))]
    face_bits = [1 << b for b in reversed(range(faces.bit_length() - 1))]
    barrier = pltpu.get_barrier_semaphore()
    for bit in tile_bits:
        pl.semaphore_signal(barrier, inc=1, device_id=(face, flipped_bit(tile, bit)), device_id_type=MESH_ID)
    for bit in face_bits:
        pl.semaphore_signal(barrier, inc=1, device_id=(flipped_bit(face, bit), tile), device_id_type=MESH_ID)
    we_all[face, tile] = we_ref[...]
    if summed:
        total[...] = sum_ref[...]

    @pl.when(tile == 0)
    def _():
        ns_all[face, 0] = ns_ref[0]

    @pl.when(tile == tiles - 1)
    def _():
        ns_all[face, 1] = ns_ref[1]

    pl.semaphore_wait(barrier, len(tile_bits) + len(face_bits))

    def share_sum(i, partner):
        if not summed:
            return None
        copy = pltpu.make_async_remote_copy(
            total, landed.at[i], ssend.at[i], srecv.at[i], partner, MESH_ID
        )
        copy.start()
        return copy

    def take_sum(i, copy):
        if summed:
            copy.wait()
            total[...] = total[...] + landed[i]

    held = [tile]
    slot = 0
    for i, bit in enumerate(tile_bits):
        partner = (face, flipped_bit(tile, bit))
        copies = []
        for h in held:
            block = we_all.at[face, h]
            copies.append(pltpu.make_async_remote_copy(block, block, wsend.at[slot], wrecv.at[slot], partner, MESH_ID))
            slot += 1
        for copy in copies:
            copy.start()
        lines = []
        for side, place in enumerate((tile, tiles - 1 - tile)):
            line = ns_all.at[face, side]
            send = pltpu.make_async_remote_copy(
                line, line, nsend.at[side, i], nrecv.at[side, i], partner, MESH_ID
            )
            place = lax.rem(place, 2 * bit)
            lines.append((place, send))

            @pl.when(place == 0)
            def _():
                send.start()

        summing = share_sum(i, partner)
        for copy in copies:
            copy.wait()
        for place, send in lines:

            @pl.when(place == 0)
            def _():
                send.wait_send()

            @pl.when(place == bit)
            def _():
                send.wait_recv()

        take_sum(i, summing)
        held = held + [flipped_bit(h, bit) for h in held]

    held = [face]
    slot = 0
    for i, bit in enumerate(face_bits):
        partner = (flipped_bit(face, bit), tile)
        copies = []
        for h in held:
            for part in (we_all.at[h], ns_all.at[h]):
                copies.append(pltpu.make_async_remote_copy(part, part, fsend.at[slot], frecv.at[slot], partner, MESH_ID))
                slot += 1
        for copy in copies:
            copy.start()
        summing = share_sum(len(tile_bits) + i, partner)
        for copy in copies:
            copy.wait()
        take_sum(len(tile_bits) + i, summing)
        held = held + [flipped_bit(h, bit) for h in held]


def gather_lines(we, ns, addend):
    faces, tiles = lax.axis_size("face"), lax.axis_size("tile")
    steps = tiles.bit_length() - 1
    every = steps + faces.bit_length() - 1
    dma = pltpu.SemaphoreType.DMA
    summed = addend is not None
    operands = [we, ns]
    outs = [
        jax.ShapeDtypeStruct((faces, tiles) + we.shape, BF16),
        jax.ShapeDtypeStruct((faces,) + ns.shape, BF16),
    ]
    scratch = [
        dma((tiles,)), dma((tiles,)), dma((2, steps)), dma((2, steps)), dma((2 * faces,)), dma((2 * faces,)),
    ]
    if summed:
        operands.append(addend)
        outs.append(jax.ShapeDtypeStruct(addend.shape, F32))
        scratch += [pltpu.VMEM((every,) + addend.shape, F32), dma((every,)), dma((every,))]
    return pl.pallas_call(
        functools.partial(gather_kernel, faces, tiles, summed),
        in_specs=[pl.BlockSpec(memory_space=pltpu.VMEM)] * len(operands),
        out_specs=[pl.BlockSpec(memory_space=pltpu.VMEM)] * len(outs),
        out_shape=outs,
        scratch_shapes=scratch,
        compiler_params=pltpu.CompilerParams(collective_id=int(summed), has_side_effects=True),
    )(*operands)


def pick_kernel(links_ref, we_ref, ns_ref, out_ref):
    tiles, channels, side = we_ref.shape[1:]
    faces_dev = ns_ref.shape[2]
    seg = side // tiles
    lane = lax.broadcasted_iota(jnp.int32, (channels, side), 1)
    column = lax.broadcasted_iota(jnp.int32, (side, side), 1)
    row = lax.broadcasted_iota(jnp.int32, (side, side), 0)
    mirror = (row + column == side - 1).astype(F32).astype(BF16)

    def pick(j, carry):
        face, edge, flip = links_ref[3 * j], links_ref[3 * j + 1], links_ref[3 * j + 2]
        group, local = lax.div(face, faces_dev), lax.rem(face, faces_dev)
        straight = ns_ref[group, jnp.minimum(edge, 1), local].astype(F32)
        offset = (local * 2 + jnp.maximum(edge - 2, 0)) * seg
        across = jnp.zeros((channels, side), F32)
        for t in range(tiles):
            moved = pltpu.roll(we_ref[group, t].astype(F32), lax.rem(t * seg - offset + side, side), 1)
            across = jnp.where((lane >= t * seg) & (lane < (t + 1) * seg), moved, across)
        line = jnp.where(edge < 2, straight, across)
        turned = jnp.dot(line.astype(BF16), mirror, preferred_element_type=F32)
        out_ref[j] = jnp.where(flip == 1, turned, line).astype(BF16)
        return carry

    lax.fori_loop(0, out_ref.shape[0], pick, 0)


def exchange(north, south, west, east, links, addend=None):
    faces_dev, channels, side = north.shape
    seg = west.shape[2]
    we = jnp.concatenate([e[f] for f in range(faces_dev) for e in (west, east)], axis=1)
    we = jnp.pad(we, ((0, 0), (0, side - 2 * faces_dev * seg)))
    gathered = gather_lines(we, jnp.stack([north, south]), addend)
    vmem = pl.BlockSpec(memory_space=pltpu.VMEM)
    ghosts = pl.pallas_call(
        pick_kernel,
        in_specs=[pl.BlockSpec(memory_space=pltpu.SMEM), vmem, vmem],
        out_specs=vmem,
        out_shape=jax.ShapeDtypeStruct((faces_dev * 4, channels, side), BF16),
    )(links.reshape(-1), gathered[0], gathered[1])
    ghosts = ghosts.reshape(faces_dev, 4, channels, side)
    return ghosts, (gathered[2] if addend is not None else None)


def halo(first, last):
    count = lax.axis_size("tile")
    down = [(i, i + 1) for i in range(count - 1)]
    up = [(i + 1, i) for i in range(count - 1)]
    return lax.ppermute(last, "tile", down), lax.ppermute(first, "tile", up)


def fill(north, south, west, east, links, corners, pos, count):
    seg = west.shape[2]
    above, below = halo(north, south)
    ghosts, _ = exchange(north, south, west, east, links)
    code = (corners == 0)[:, :, None]
    gn, gs, gw, ge = (ghosts[:, i] for i in range(4))
    nw = jnp.where(code[:, 0], gn[:, :, 0], gw[:, :, 0])
    ne = jnp.where(code[:, 1], gn[:, :, -1], ge[:, :, 0])
    sw = jnp.where(code[:, 2], gs[:, :, 0], gw[:, :, -1])
    se = jnp.where(code[:, 3], gs[:, :, -1], ge[:, :, -1])
    west_all = jnp.concatenate([nw[:, :, None], gw, sw[:, :, None]], axis=2)
    east_all = jnp.concatenate([ne[:, :, None], ge, se[:, :, None]], axis=2)
    columns = jnp.stack([west_all, east_all], axis=1)
    columns = lax.dynamic_slice_in_dim(columns, pos * seg, seg + 2, 3).astype(F32)
    columns = jnp.pad(columns, ((0, 0), (0, 0), (0, 0), (0, LANES - seg - 2)))
    top = jnp.where(pos == 0, gn, above)
    bottom = jnp.where(pos == count - 1, gs, below)
    return jnp.stack([top, bottom], axis=1), columns


def line_product(weights, line):
    size = line.shape[2]
    padded = jnp.pad(line, ((0, 0), (0, 0), (2, 2)))
    stacked = jnp.concatenate([padded[:, :, 2 - t : 2 - t + size + 2] for t in range(3)], axis=1)
    flat = jnp.transpose(weights, (2, 0, 1)).reshape(-1, weights.shape[1])
    return jnp.einsum("kc,fkq->fcq", flat, stacked, preferred_element_type=F32)


def unfold_edges(north, south, west, east, weight, links, corners, pos, count, addend):
    seg = west.shape[2]
    above, below = halo(north, south)
    rows = jnp.stack([above, below], axis=1)
    west = jnp.concatenate([above[:, :, :1], west, below[:, :, :1]], axis=2)
    east = jnp.concatenate([above[:, :, -1:], east, below[:, :, -1:]], axis=2)
    gn = line_product(weight[:, :, 0, :], north)
    gs = line_product(weight[:, :, 2, :], south)
    gw = line_product(weight[:, :, :, 0], west)[:, :, 2:-2]
    ge = line_product(weight[:, :, :, 2], east)[:, :, 2:-2]
    code = corners[:, :, None]
    zero = jnp.zeros((), F32)
    at_top, at_bottom = pos == 0, pos == count - 1
    nw, ne, sw, se = gn[:, :, :1], gn[:, :, -1:], gs[:, :, :1], gs[:, :, -1:]
    keep = lambda i, corner: jnp.where(code[:, i, :, None] == 0, corner, zero)
    give = lambda i, corner, here: jnp.where((code[:, i, :, None] == 1) & here, corner, zero)
    ends = lambda lo, hi, n: jnp.pad(lo, ((0, 0), (0, 0), (0, n - 1))) + jnp.pad(hi, ((0, 0), (0, 0), (n - 1, 0)))
    side = north.shape[2]
    gn_line = gn[:, :, 1:-1] + ends(keep(0, nw), keep(1, ne), side)
    gs_line = gs[:, :, 1:-1] + ends(keep(2, sw), keep(3, se), side)
    gw_line = gw + ends(give(0, nw, at_top), give(2, sw, at_bottom), seg)
    ge_line = ge + ends(give(1, ne, at_top), give(3, se, at_bottom), seg)
    ghosts, total = exchange(
        gn_line.astype(BF16), gs_line.astype(BF16), gw_line.astype(BF16), ge_line.astype(BF16), links, addend
    )
    ghosts = ghosts.astype(F32)
    columns = lax.dynamic_slice_in_dim(ghosts[:, 2:], pos * seg, seg, 3)
    columns = jnp.pad(columns, ((0, 0), (0, 0), (0, 0), (0, LANES - seg)))
    edges = jnp.stack(
        [jnp.where(at_top, ghosts[:, 0], zero), jnp.where(at_bottom, ghosts[:, 1], zero)], axis=1
    )
    return rows, columns, edges, total


def body(field_in, out_grad, weight_first, bias_first, weight_second, bias_second, face_links, corner_rules):
    count = lax.axis_size("tile")
    pos = lax.axis_index("tile")
    face_pos = lax.axis_index("face")
    faces, channels, rows, side = field_in.shape
    links = lax.dynamic_slice_in_dim(face_links, face_pos * faces, faces, 0)
    corners = lax.dynamic_slice_in_dim(corner_rules, face_pos * faces, faces, 0)
    swap = lambda a: jnp.transpose(a, (0, 2, 1, 3))
    ahead = lambda w: jnp.transpose(w, (0, 2, 3, 1)).reshape(channels, 9 * channels)
    behind = lambda w: jnp.transpose(w[:, :, ::-1, ::-1], (1, 2, 3, 0)).reshape(channels, 9 * channels)
    flops = 2 * 9 * channels * channels * faces * rows * side
    full = (faces, rows, channels, side)
    edge_out = ((faces, 2, channels, LANES), F32)
    sums = [((9 * channels, channels), F32), ((channels, side), F32)]

    x = swap(field_in)
    og = swap(out_grad)
    xhalo, xghost = fill(
        field_in[:, :, 0], field_in[:, :, -1], field_in[:, :, :, 0], field_in[:, :, :, -1],
        links, corners, pos, count,
    )
    hidden, slope, hedge = run_faces(
        first_kernel, [x, xhalo, xghost], [ahead(weight_first), bias_first[:, None]],
        [(full, BF16), (full, F32), edge_out], [], 1, flops,
    )

    def sides(edge):
        return edge[:, 0, :, :rows].astype(BF16), edge[:, 1, :, :rows].astype(BF16)

    depth = 9 * channels

    def packed(gw, gb):
        both = jnp.concatenate([gw.T, jnp.sum(gb, axis=1, keepdims=True)], axis=1)
        return jnp.pad(both, ((0, 0), (0, -both.shape[1] % LANES)))

    hhalo, hghost = fill(hidden[:, 0], hidden[:, -1], *sides(hedge), links, corners, pos, count)
    output, g2, gedge, gw2, gb2 = run_faces(
        second_kernel, [hidden, hhalo, hghost, og], [ahead(weight_second), bias_second[:, None]],
        [(full, BF16), (full, BF16), edge_out], sums, 1, 2 * flops,
    )
    ghalo, gcol, grow, sum2 = unfold_edges(
        g2[:, 0], g2[:, -1], *sides(gedge), weight_second, links, corners, pos, count, packed(gw2, gb2)
    )
    g1, fedge, gw1, gb1 = run_faces(
        third_kernel, [g2, ghalo, gcol, grow, slope, x, xhalo, xghost], [behind(weight_second)],
        [(full, BF16), edge_out], sums, 2, 2 * flops,
    )
    fhalo, fcol, frow, sum1 = unfold_edges(
        g1[:, 0], g1[:, -1], *sides(fedge), weight_first, links, corners, pos, count, packed(gw1, gb1)
    )
    (grad_field,) = run_faces(
        fourth_kernel, [g1, fhalo, fcol, frow], [behind(weight_first)], [(full, BF16)], [], 1, flops
    )
    shaped = lambda g: jnp.transpose(g[:, :depth].reshape(channels, 3, 3, channels), (0, 3, 1, 2)) / side
    return (
        swap(output),
        swap(grad_field),
        shaped(sum1),
        sum1[:, depth] / side,
        shaped(sum2),
        sum2[:, depth] / side,
    )


def solution(mesh):
    cells = P("face", None, "tile", None)
    return jax.shard_map(
        body,
        mesh=mesh,
        in_specs=(cells, cells, P(), P(), P(), P(), P(), P()),
        out_specs=(cells, cells, P(), P(), P(), P()),
        check_vma=False,
    )
```
